256 devices in a mesh: outer: 8 (over y, x_hi), inner: 32 (over x_lo, z, core).
Axes of the slice: x: 4 (x_hi: 2, x_lo: 2; x = x_hi * 2 + x_lo), y: 4, z: 8, core: 2. Of those that a mesh axis runs over, the one named last changes fastest.
Arguments:
- ratings: bfloat16 [262144, 2048], P(('outer', 'inner')), may hold values from -4 to 4
- rating_weights: bfloat16 [262144, 2048], P(('outer', 'inner')), may hold values from 0 to 1.5, as said below
- user_counts: int32 [262144], P(('outer', 'inner')), may hold values from 16 to 96
- item_counts: int32 [65536], replicated, may hold values from 32 to 256
- users: bfloat16 [262144, 256], P(('outer', 'inner')), may hold values from -1.5 to 1.5
- user_moment: float32 [262144, 256], P(('outer', 'inner')), may hold values from -0.3 to 0.3
- items: bfloat16 [65536, 256], P(('outer', 'inner')), may hold values from -1.5 to 1.5
- item_moment: bfloat16 [65536, 256], P(('outer', 'inner')), may hold values from -0.29882812 to 0.29882812
Outputs:
- new_users: bfloat16 [262144, 256], P(('outer', 'inner'))
- new_user_moment: float32 [262144, 256], P(('outer', 'inner'))
- new_items: bfloat16 [65536, 256], P(('outer', 'inner'))
- new_item_moment: bfloat16 [65536, 256], P(('outer', 'inner'))
The draws below stay inside these ranges and needn't reach their ends.
Inputs may be any that keep to these rules, and one draw needn't show every extreme that they name: `rating_weights`: A weight is 0 exactly where the rating is not observed, else positive.
All inputs are finite; a program needn't handle non-finite values.
Results may differ from the reference program's by a relative error of at most 0.011.
Values may be sent and summed in bfloat16 or wider, within the bound.
No kernel may reach another device: no remote copies, remote signals or barrier semaphores. Data moves between devices by JAX's collectives and lax.ppermute only.
A program may use at most 128 MiB of HBM per device.

```python
import jax
import jax.numpy as jnp
from jax import lax

NU = 1024
R = 256
IB = 256
STEPS = 8
USERS = 262144
ITEMS = 65536
N_OUTER = 8
N_INNER = 32


def draw_rating_weights(key, part):
    width = STEPS * IB
    observed = (jax.random.randint(jax.random.fold_in(key, 31), (USERS, width), 0, 8) == 0).astype(jnp.float32)
    level = jax.random.uniform(jax.random.fold_in(key, 47), (USERS, width), jnp.float32, 0.5, 1.5)
    return (observed * level).astype(jnp.bfloat16)


def touch_ends(result, own_key, smallest, top_value):
    spot = [jax.random.randint(jax.random.fold_in(own_key, axis), (), 0, length) for axis, length in enumerate(result.shape)]
    main_axis = result.shape.index(max(result.shape))
    beside = spot[:main_axis] + [(spot[main_axis] + 1) % result.shape[main_axis]] + spot[main_axis + 1:]
    return result.at[tuple(spot)].set(smallest).at[tuple(beside)].set(top_value)


def levels(own_key, dims, cuts, least, largest):
    gain = 1.0
    for axis_at, parts in cuts:
        heights = jax.random.uniform(jax.random.fold_in(jax.random.fold_in(own_key, 6), axis_at), (parts,), jnp.float32, least / len(cuts), largest / len(cuts))
        gain = gain * jnp.repeat(jnp.exp(heights), dims[axis_at] // parts).reshape((-1,) + (1,) * (len(dims) - 1 - axis_at))
    return gain


def noise(rng, shape, scale, most, cuts=(), held_as=jnp.bfloat16):
    values = scale * jax.random.normal(rng, shape, jnp.float32)
    if cuts:
        values = values * levels(rng, shape, cuts, -0.22, 0.18)
    return jnp.clip(values, -most, most).astype(held_as)


def setup_inputs(seed: int = 0) -> dict:
    seeds = jax.random.split(jax.random.key(seed), 9)
    return {
        "ratings": noise(seeds[0], (USERS, STEPS * IB), 1.0, 4.0, ((0, 256),)),
        "rating_weights": draw_rating_weights(jax.random.fold_in(seeds[8], 71), 0),
        "user_counts": touch_ends(jax.random.randint(seeds[2], (USERS,), 16, 97), jax.random.fold_in(seeds[2], 1), 16, 96).astype(jnp.int32),
        "item_counts": touch_ends(jax.random.randint(seeds[3], (ITEMS,), 32, 257), jax.random.fold_in(seeds[3], 1), 32, 256).astype(jnp.int32),
        "users": noise(seeds[4], (USERS, R), 0.25, 1.5, ((0, 256),)),
        "user_moment": noise(seeds[5], (USERS, R), 0.05, 0.3, ((0, 256),), jnp.float32),
        "items": noise(seeds[6], (ITEMS, R), 0.25, 1.5, ((0, 256),)),
        "item_moment": noise(seeds[7], (ITEMS, R), 0.05, 0.29882812, ((0, 256),)),
    }


learn_rate = 0.3
moment_rate = 0.9
decay_rate = 0.02


def misfit_of(users, items, rated, weight):
    predicted = jnp.dot(users, items.T, preferred_element_type=jnp.float32)
    return (weight * (predicted - rated.astype(jnp.float32))).astype(jnp.bfloat16)


def item_step(misfit, users, items, moment, counts):
    product = lax.dot_general(misfit, users, (((0,), (0,)), ((), ())), preferred_element_type=jnp.float32)
    grad = product / counts[:, None] + decay_rate * items.astype(jnp.float32)
    moment_new = (moment_rate * moment.astype(jnp.float32) + grad).astype(jnp.bfloat16)
    kept = lax.optimization_barrier(moment_new)
    items_new = (items.astype(jnp.float32) - learn_rate * kept.astype(jnp.float32)).astype(jnp.bfloat16)
    return items_new, moment_new


def user_step(grad_sum, users, moment, counts):
    grad = grad_sum / counts[:, None] + decay_rate * users.astype(jnp.float32)
    moment_new = moment_rate * moment + grad
    users_new = (users.astype(jnp.float32) - learn_rate * moment_new).astype(jnp.bfloat16)
    return users_new, moment_new


def reference(ratings, rating_weights, user_counts, item_counts, users, user_moment, items, item_moment):
    devices = N_OUTER * N_INNER
    rated_all = ratings.reshape(devices, NU, STEPS, IB)
    weight_all = rating_weights.reshape(devices, NU, STEPS, IB)
    ucount = user_counts.reshape(devices, NU).astype(jnp.float32)
    icount = item_counts.reshape(devices, IB).astype(jnp.float32)
    user_blocks = users.reshape(devices, NU, R)
    user_moms = user_moment.reshape(devices, NU, R)
    item_blocks = items.reshape(devices, IB, R)
    item_moms = item_moment.reshape(devices, IB, R)
    block_ids = jnp.arange(devices, dtype=jnp.int32)
    for step in range(STEPS):
        def one_device(packed):
            ublock, umom, iblock, imom, rated, weight, ucnt, icnt = packed
            misfit = misfit_of(ublock, iblock, rated, weight.astype(jnp.float32))
            new_items, new_imom = item_step(misfit, ublock, iblock, imom, icnt)
            grad_sum = jnp.dot(misfit, iblock, preferred_element_type=jnp.float32)
            new_users, new_umom = user_step(grad_sum, ublock, umom, ucnt)
            return new_users, new_umom, new_items, new_imom

        user_blocks, user_moms, item_blocks, item_moms = lax.map(one_device, (user_blocks, user_moms, item_blocks, item_moms, rated_all[:, :, step], weight_all[:, :, step], ucount, icount[block_ids]))
        if step < STEPS - 1:
            axis_used = 0 if step == STEPS // 2 - 1 else 1
            item_blocks = jnp.roll(item_blocks.reshape(N_OUTER, N_INNER, IB, R), 1, axis=axis_used).reshape(devices, IB, R)
            item_moms = jnp.roll(item_moms.reshape(N_OUTER, N_INNER, IB, R), 1, axis=axis_used).reshape(devices, IB, R)
            block_ids = jnp.roll(block_ids.reshape(N_OUTER, N_INNER), 1, axis=axis_used).reshape(devices)
    return (user_blocks.reshape(USERS, R), user_moms.reshape(USERS, R), item_blocks.reshape(ITEMS, R), item_moms.reshape(ITEMS, R))
```

```python
import functools

import jax
import jax.numpy as jnp
from jax import lax
from jax.experimental import pallas as pl
from jax.experimental.pallas import tpu as pltpu
from jax.sharding import PartitionSpec as P

STEPS = 8
ODD_PIECES = 1
EVEN_PIECES = 2
LANES = 128
ROW_CHUNKS = 4

learn_rate = 0.3
moment_rate = 0.9
decay_rate = 0.02

f32 = jnp.float32
bf16 = jnp.bfloat16
VMEM = pltpu.MemorySpace.VMEM
HBM = pltpu.MemorySpace.HBM


def ring(count):
    return [(i, (i + 1) % count) for i in range(count)]


def swap(count):
    return [(i, i ^ 1) for i in range(count)]


def shifted(block, axis, pairs):
    return [lax.ppermute(piece, axis, pairs) for piece in block]


def hbm(array):
    return pltpu.with_memory_space_constraint(array, HBM), HBM


def kernel_call(kernel, ins, outs, aliases, scratch=()):
    names = list(ins) + ["out_" + n for n in outs] + [n for n, _ in scratch]

    def wrapped(*refs):
        kernel(dict(zip(names, refs)))

    in_names, out_names = list(ins), list(outs)
    res = pl.pallas_call(
        wrapped,
        out_shape=[jax.ShapeDtypeStruct(v[0].shape, v[0].dtype) for v in outs.values()],
        in_specs=[pl.BlockSpec(memory_space=v[1]) for v in ins.values()],
        out_specs=[pl.BlockSpec(memory_space=v[1]) for v in outs.values()],
        scratch_shapes=[s for _, s in scratch],
        input_output_aliases={in_names.index(a): out_names.index(b) for a, b in aliases.items()},
        compiler_params=pltpu.CompilerParams(vmem_limit_bytes=32 * 1024 * 1024),
        cost_estimate=pl.CostEstimate(flops=1000, bytes_accessed=1000, transcendentals=0),
    )(*[v[0] for v in ins.values()])
    return dict(zip(out_names, res))


def parity():
    return lax.rem(lax.axis_index("inner"), 2)


def anchor_of(step):
    n_outer, n_inner = lax.axis_size("outer"), lax.axis_size("inner")
    late = 1 if step >= STEPS // 2 else 0
    outer = lax.rem(lax.axis_index("outer") + (n_outer - late), n_outer)
    inner = lax.rem(lax.axis_index("inner") + (n_inner - (step - late)), n_inner)
    return outer * n_inner + inner


def table_copies(r, step, width):
    cols = pl.ds(step * width, width)
    group = pl.multiple_of(lax.div(anchor_of(step), 4) * 8, 8)
    return [
        pltpu.make_async_copy(r["ratings"].at[:, cols], r["out_xs"], r["sem"].at[0]),
        pltpu.make_async_copy(r["weights"].at[:, cols], r["out_ws"], r["sem"].at[1]),
        pltpu.make_async_copy(r["icount"].at[pl.ds(group, 8), :], r["out_cg"], r["sem"].at[2]),
    ]


def item_part(step, u, ut, vt, qt, xs, ws, cg, m, new):
    rows = u.shape[0] // ROW_CHUNKS
    for k in range(ROW_CHUNKS):
        part = slice(k * rows, (k + 1) * rows)
        pred = jnp.dot(u[part, :], vt, preferred_element_type=f32)
        m[part, :] = (ws[part, :].astype(f32) * (pred - xs[part, :].astype(f32))).astype(bf16)
    product = jnp.dot(ut[...], m[...], preferred_element_type=f32)
    pair = cg[pl.ds(lax.rem(anchor_of(step), 4) * 2, 2), :].astype(f32)
    inverse = 1.0 / jnp.concatenate([pair[0:1, :], pair[1:2, :]], axis=1)
    grad = product * inverse + decay_rate * vt.astype(f32)
    q_new = (moment_rate * qt.astype(f32) + grad).astype(bf16)
    v_new = (vt.astype(f32) - learn_rate * q_new.astype(f32)).astype(bf16)
    put(new, v_new, q_new)


def user_rows(part, vt, u, p, m, rc):
    total = lax.dot_general(
        m[part, :], vt, (((1,), (1,)), ((), ())), preferred_element_type=f32
    )
    old = u[part, :].astype(f32)
    scale = jnp.concatenate([rc[part, :]] * (total.shape[1] // LANES), axis=1)
    p_new = moment_rate * p[part, :] + (total * scale + decay_rate * old)
    return p_new, (old - learn_rate * p_new).astype(bf16)


def put(block, vt, qt):
    if len(block) == 1:
        block[0][: vt.shape[0], :] = vt
        block[0][vt.shape[0] :, :] = qt
        return
    half = len(block) // 2
    span = vt.shape[0] // half
    for k in range(half):
        block[k][...] = vt[k * span : (k + 1) * span]
        block[half + k][...] = qt[k * span : (k + 1) * span]


def factors(block):
    if len(block) == 1:
        return block[0][: block[0].shape[0] // 2, :]
    return jnp.concatenate([ref[...] for ref in block[: len(block) // 2]], axis=0)


def momentum(block):
    if len(block) == 1:
        return block[0][block[0].shape[0] // 2 :, :]
    return jnp.concatenate([ref[...] for ref in block[len(block) // 2 :]], axis=0)


STATE = ("u", "ut", "p", "m", "xs", "ws", "cg", "rc")


def pieces(r, name):
    return [r[name + str(k)] for k in range(2 * len(r)) if name + str(k) in r]


def init_kernel(width, r):
    copies = [
        pltpu.make_async_copy(r["items"], r["v"], r["sem"].at[3]),
        pltpu.make_async_copy(r["users"], r["out_u"], r["sem"].at[4]),
        *table_copies(r, 0, width),
        pltpu.make_async_copy(r["imom"], r["q"], r["sem"].at[5]),
        pltpu.make_async_copy(r["umom"], r["out_p"], r["sem"].at[6]),
    ]
    for c in copies:
        c.start()
    items, users, xs, ws, cg, imom, umom = copies
    items.wait()
    vt = r["v"][...].T
    users.wait()
    r["out_ut"][...] = r["out_u"][...].T
    imom.wait()
    qt = r["q"][...].T
    first = pieces(r, "out_first")
    put(first, vt, qt)
    xs.wait()
    ws.wait()
    cg.wait()
    new = pieces(r, "out_new")

    @pl.when(parity() == 1)
    def _():
        item_part(
            0, r["out_u"], r["out_ut"], factors(first), momentum(first),
            r["out_xs"], r["out_ws"], r["out_cg"], r["out_m"], new,
        )

    umom.wait()


def phase_kernel(width, item_parity, item_step, user_step, r):
    if item_step is not None:

        @pl.when(parity() == item_parity)
        def _():
            blk = pieces(r, "blk")
            item_part(
                item_step, r["u"], r["ut"], factors(blk), momentum(blk),
                r["xs"], r["ws"], r["cg"], r["out_m"], pieces(r, "out_new"),
            )

    if user_step is not None:

        @pl.when(parity() == 1 - item_parity)
        def _():
            copies = table_copies(r, user_step + 1, width) if user_step + 1 < STEPS else []
            for c in copies:
                c.start()
            if user_step == 0:
                inverse = 1.0 / r["ucount"][...].astype(f32)
                for k in range(inverse.shape[0]):
                    row = jnp.broadcast_to(inverse[k : k + 1, :], (LANES, LANES))
                    r["out_rc"][k * LANES : (k + 1) * LANES, :] = row.T
            vt = factors(pieces(r, "vold"))
            rows = r["u"].shape[0] // ROW_CHUNKS
            for k in range(ROW_CHUNKS):
                part = slice(k * rows, (k + 1) * rows)
                p_new, u_new = user_rows(part, vt, r["u"], r["p"], r["m"], r["out_rc"])
                r["out_p"][part, :] = p_new
                r["out_u"][part, :] = u_new
                r["out_ut"][:, part] = u_new.T
            for c in copies:
                c.wait()


def final_kernel(width, r):
    def items_out(block):
        r["v"][...] = factors(block).T
        r["q"][...] = momentum(block).T
        return [
            pltpu.make_async_copy(r["v"], r["out_items"], r["sem"].at[0]),
            pltpu.make_async_copy(r["q"], r["out_imom"], r["sem"].at[1]),
        ]

    rows = r["u"].shape[0] // ROW_CHUNKS

    def rows_out(k, u, p):
        part = pl.ds(k * rows, rows)
        return [
            pltpu.make_async_copy(u.at[part, :], r["out_users"].at[part, :], r["sem"].at[2 + 2 * k]),
            pltpu.make_async_copy(p.at[part, :], r["out_umom"].at[part, :], r["sem"].at[3 + 2 * k]),
        ]

    @pl.when(parity() == 1)
    def _():
        copies = [c for k in range(ROW_CHUNKS) for c in rows_out(k, r["u"], r["p"])]
        for c in copies:
            c.start()
        late = items_out(pieces(r, "odd"))
        for c in late:
            c.start()
        for c in copies + late:
            c.wait()

    @pl.when(parity() == 0)
    def _():
        copies = items_out(pieces(r, "even"))
        for c in copies:
            c.start()
        vt = factors(pieces(r, "vold"))
        for k in range(ROW_CHUNKS):
            part = slice(k * rows, (k + 1) * rows)
            p_new, u_new = user_rows(part, vt, r["u"], r["p"], r["m"], r["rc"])
            r["ps"][part, :] = p_new
            r["us"][part, :] = u_new
            some = rows_out(k, r["us"], r["ps"])
            for c in some:
                c.start()
            copies += some
        for c in copies:
            c.wait()


def body(ratings, rating_weights, user_counts, item_counts, users, user_moment, items, item_moment):
    n_outer = lax.axis_size("outer")
    n_inner = lax.axis_size("inner")
    width, rank = items.shape
    n_users = users.shape[0]
    block_of = lambda n: [jax.ShapeDtypeStruct((2 * rank // n, width), bf16)] * n
    icount = item_counts.reshape(-1, LANES)
    ucount = user_counts.reshape(-1, LANES)
    shapes = {
        "u": jax.ShapeDtypeStruct((n_users, rank), bf16),
        "ut": jax.ShapeDtypeStruct((rank, n_users), bf16),
        "p": jax.ShapeDtypeStruct((n_users, rank), f32),
        "m": jax.ShapeDtypeStruct((n_users, width), bf16),
        "xs": jax.ShapeDtypeStruct((n_users, width), bf16),
        "ws": jax.ShapeDtypeStruct((n_users, width), bf16),
        "cg": jax.ShapeDtypeStruct((8, LANES), jnp.int32),
        "rc": jax.ShapeDtypeStruct((n_users, LANES), f32),
    }
    numbered = lambda name, block: {name + str(k): (b, VMEM) for k, b in enumerate(block)}
    listed = lambda res, name: [res[name + str(k)] for k in range(len(res)) if name + str(k) in res]
    tables = {"ratings": hbm(ratings), "weights": hbm(rating_weights), "icount": hbm(icount)}

    res = kernel_call(
        functools.partial(init_kernel, width),
        {
            **tables,
            "users": hbm(users), "umom": hbm(user_moment),
            "items": hbm(items), "imom": hbm(item_moment),
        },
        {
            **{n: (s, VMEM) for n, s in shapes.items()},
            **numbered("first", block_of(1)), **numbered("new", block_of(ODD_PIECES)),
        },
        {},
        [
            ("v", pltpu.VMEM((width, rank), bf16)),
            ("q", pltpu.VMEM((width, rank), bf16)),
            ("sem", pltpu.SemaphoreType.DMA((7,))),
        ],
    )
    state = {n: res[n] for n in STATE}
    odd_blk = even_blk = listed(res, "first")
    odd_new = listed(res, "new")

    def phase(item_parity, item_step, user_step, state, blk, vold):
        sends_outer = item_step == STEPS // 2 - 1
        count = ODD_PIECES if item_parity == 1 or sends_outer else EVEN_PIECES
        ins = {n: (state[n], VMEM) for n in STATE}
        ins.update(tables)
        ins["ucount"] = (ucount, VMEM)
        ins.update(numbered("blk", blk))
        ins.update(numbered("vold", vold))
        outs = {n: (shapes[n], VMEM) for n in STATE}
        outs.update(numbered("new", block_of(count)))
        res = kernel_call(
            functools.partial(phase_kernel, width, item_parity, item_step, user_step),
            ins, outs, {n: n for n in STATE},
            [("sem", pltpu.SemaphoreType.DMA((3,)))],
        )
        return {n: res[n] for n in STATE}, listed(res, "new")

    for step in range(STEPS):
        if step > 0:
            state, odd_new = phase(1, step, step - 1, state, odd_blk, even_old)
        if step == STEPS // 2 - 1:
            odd_sent = shifted(odd_new, "outer", ring(n_outer))
        elif step < STEPS - 1:
            odd_sent = shifted(odd_new, "inner", ring(n_inner))
        state, even_new = phase(0, step, step, state, even_blk, odd_blk)
        even_old = even_blk
        if step == STEPS // 2 - 1:
            odd_blk, even_blk = odd_sent, shifted(even_new, "outer", ring(n_outer))
        elif step < STEPS - 1:
            odd_blk, even_blk = shifted(even_new, "inner", swap(n_inner)), odd_sent

    res = kernel_call(
        functools.partial(final_kernel, width),
        {
            **{n: (state[n], VMEM) for n in ("u", "p", "m", "rc")},
            **numbered("odd", odd_new), **numbered("even", even_new),
            **numbered("vold", even_old),
        },
        {
            "users": (shapes["u"], HBM), "umom": (shapes["p"], HBM),
            "items": (items, HBM), "imom": (items, HBM),
        },
        {},
        [
            ("v", pltpu.VMEM((width, rank), bf16)),
            ("q", pltpu.VMEM((width, rank), bf16)),
            ("us", pltpu.VMEM((n_users, rank), bf16)),
            ("ps", pltpu.VMEM((n_users, rank), f32)),
            ("sem", pltpu.SemaphoreType.DMA((2 + 2 * ROW_CHUNKS,))),
        ],
    )
    return (res["users"], res["umom"], res["items"], res["imom"])


def solution(mesh):
    in_specs = (
        P(("outer", "inner"), None),
        P(("outer", "inner"), None),
        P(("outer", "inner")),
        P(),
        P(("outer", "inner"), None),
        P(("outer", "inner"), None),
        P(("outer", "inner"), None),
        P(("outer", "inner"), None),
    )
    out_specs = (
        P(("outer", "inner"), None),
        P(("outer", "inner"), None),
        P(("outer", "inner"), None),
        P(("outer", "inner"), None),
    )
    return jax.shard_map(body, mesh=mesh, in_specs=in_specs, out_specs=out_specs, check_vma=False)
```

```python
import functools

import jax
import jax.numpy as jnp
from jax import lax
from jax.experimental import pallas as pl
from jax.experimental.pallas import tpu as pltpu
from jax.sharding import PartitionSpec as P

STEPS = 8
ODD_PIECES = 1
EVEN_PIECES = 2
USER_FLOPS = 1000
LANES = 128
ROW_CHUNKS = 4

learn_rate = 0.3
moment_rate = 0.9
decay_rate = 0.02

f32 = jnp.float32
bf16 = jnp.bfloat16
VMEM = pltpu.MemorySpace.VMEM
HBM = pltpu.MemorySpace.HBM


def ring(count):
    return [(i, (i + 1) % count) for i in range(count)]


def swap(count):
    return [(i, i ^ 1) for i in range(count)]


def shifted(block, axis, pairs):
    return [lax.ppermute(piece, axis, pairs) for piece in block]


def hbm(array):
    return pltpu.with_memory_space_constraint(array, HBM), HBM


def kernel_call(kernel, ins, outs, aliases, scratch=(), flops=1000):
    names = list(ins) + ["out_" + n for n in outs] + [n for n, _ in scratch]

    def wrapped(*refs):
        kernel(dict(zip(names, refs)))

    in_names, out_names = list(ins), list(outs)
    res = pl.pallas_call(
        wrapped,
        out_shape=[jax.ShapeDtypeStruct(v[0].shape, v[0].dtype) for v in outs.values()],
        in_specs=[pl.BlockSpec(memory_space=v[1]) for v in ins.values()],
        out_specs=[pl.BlockSpec(memory_space=v[1]) for v in outs.values()],
        scratch_shapes=[s for _, s in scratch],
        input_output_aliases={in_names.index(a): out_names.index(b) for a, b in aliases.items()},
        compiler_params=pltpu.CompilerParams(vmem_limit_bytes=32 * 1024 * 1024),
        cost_estimate=pl.CostEstimate(flops=flops, bytes_accessed=1000, transcendentals=0),
    )(*[v[0] for v in ins.values()])
    return dict(zip(out_names, res))


def parity():
    return lax.rem(lax.axis_index("inner"), 2)


def anchor_of(step):
    n_outer, n_inner = lax.axis_size("outer"), lax.axis_size("inner")
    late = 1 if step >= STEPS // 2 else 0
    outer = lax.rem(lax.axis_index("outer") + (n_outer - late), n_outer)
    inner = lax.rem(lax.axis_index("inner") + (n_inner - (step - late)), n_inner)
    return outer * n_inner + inner


def first_copies(r, width):
    group = pl.multiple_of(lax.div(anchor_of(0), 4) * 8, 8)
    return [
        pltpu.make_async_copy(r["ratings"].at[:, pl.ds(0, width)], r["out_xs"], r["sem"].at[0]),
        pltpu.make_async_copy(r["weights"].at[:, pl.ds(0, width)], r["out_ws"], r["sem"].at[1]),
        pltpu.make_async_copy(r["icount"].at[pl.ds(group, 8), :], r["out_cg"], r["sem"].at[2]),
    ]


def item_part(u, ut, vt, qt, xs, ws, cols, pair, m, vo, new):
    rows = u.shape[0] // ROW_CHUNKS
    for k in range(ROW_CHUNKS):
        part = slice(k * rows, (k + 1) * rows)
        pred = jnp.dot(u[part, :], vt, preferred_element_type=f32)
        x = xs[part, cols].astype(f32)
        m[part, :] = (ws[part, cols].astype(f32) * (pred - x)).astype(bf16)
    product = jnp.dot(ut[...], m[...], preferred_element_type=f32)
    pair = pair.astype(f32)
    inverse = 1.0 / jnp.concatenate([pair[0:1, :], pair[1:2, :]], axis=1)
    grad = product * inverse + decay_rate * vt.astype(f32)
    q_new = (moment_rate * qt.astype(f32) + grad).astype(bf16)
    v_new = (vt.astype(f32) - learn_rate * q_new.astype(f32)).astype(bf16)
    put(new, v_new, q_new)
    vo[...] = vt


def user_rows(part, vt, u, p, m, rc):
    total = lax.dot_general(
        m[part, :], vt, (((1,), (1,)), ((), ())), preferred_element_type=f32
    )
    old = u[part, :].astype(f32)
    scale = jnp.concatenate([rc[part, :]] * (total.shape[1] // LANES), axis=1)
    p_new = moment_rate * p[part, :] + (total * scale + decay_rate * old)
    return p_new, (old - learn_rate * p_new).astype(bf16)


def put(block, vt, qt):
    if len(block) == 1:
        block[0][: vt.shape[0], :] = vt
        block[0][vt.shape[0] :, :] = qt
        return
    half = len(block) // 2
    span = vt.shape[0] // half
    for k in range(half):
        block[k][...] = vt[k * span : (k + 1) * span]
        block[half + k][...] = qt[k * span : (k + 1) * span]


def factors(block):
    if len(block) == 1:
        return block[0][: block[0].shape[0] // 2, :]
    return jnp.concatenate([ref[...] for ref in block[: len(block) // 2]], axis=0)


def momentum(block):
    if len(block) == 1:
        return block[0][block[0].shape[0] // 2 :, :]
    return jnp.concatenate([ref[...] for ref in block[len(block) // 2 :]], axis=0)


STATE = ("u", "ut", "p", "m", "vo", "rc")


def pieces(r, name):
    return [r[name + str(k)] for k in range(2 * len(r)) if name + str(k) in r]


def init_kernel(width, r):
    copies = [
        pltpu.make_async_copy(r["items"], r["v"], r["sem"].at[3]),
        pltpu.make_async_copy(r["users"], r["out_u"], r["sem"].at[4]),
        *first_copies(r, width),
        pltpu.make_async_copy(r["imom"], r["q"], r["sem"].at[5]),
        pltpu.make_async_copy(r["umom"], r["out_p"], r["sem"].at[6]),
    ]
    for c in copies:
        c.start()
    items, users, xs, ws, cg, imom, umom = copies
    items.wait()
    vt = r["v"][...].T
    users.wait()
    r["out_ut"][...] = r["out_u"][...].T
    imom.wait()
    qt = r["q"][...].T
    first = pieces(r, "out_first")
    put(first, vt, qt)
    xs.wait()
    ws.wait()
    cg.wait()
    new = pieces(r, "out_new")

    @pl.when(parity() == 1)
    def _():
        pair = r["out_cg"][pl.ds(lax.rem(anchor_of(0), 4) * 2, 2), :]
        item_part(
            r["out_u"], r["out_ut"], factors(first), momentum(first),
            r["out_xs"], r["out_ws"], slice(0, width), pair, r["out_m"], r["out_vo"], new,
        )

    umom.wait()


def item_kernel(width, item_parity, step, r):
    @pl.when(parity() == item_parity)
    def _():
        blk = pieces(r, "blk")
        if step == 0:
            cols, pair = slice(0, width), r["cg"][pl.ds(lax.rem(anchor_of(0), 4) * 2, 2), :]
        else:
            cols = slice(step * width, (step + 1) * width)
            pair = r["cg"][pl.ds(anchor_of(step) * 2, 2), :]
        item_part(
            r["u"], r["ut"], factors(blk), momentum(blk), r["xs"], r["ws"], cols, pair,
            r["out_m"], r["out_vo"], pieces(r, "out_new"),
        )


def user_kernel(step, r):
    if step == 0:
        inverse = 1.0 / r["ucount"][...].astype(f32)
        for k in range(inverse.shape[0]):
            row = jnp.broadcast_to(inverse[k : k + 1, :], (LANES, LANES))
            r["out_rc"][k * LANES : (k + 1) * LANES, :] = row.T
    rows = r["u"].shape[0] // ROW_CHUNKS
    for k in range(ROW_CHUNKS):
        part = slice(k * rows, (k + 1) * rows)
        p_new, u_new = user_rows(part, r["vo"][...], r["u"], r["p"], r["m"], r["out_rc"] if step == 0 else r["rc"])
        r["out_p"][part, :] = p_new
        r["out_u"][part, :] = u_new
        r["out_ut"][:, part] = u_new.T


def final_kernel(width, r):
    def items_out(block):
        r["v"][...] = factors(block).T
        r["q"][...] = momentum(block).T
        return [
            pltpu.make_async_copy(r["v"], r["out_items"], r["sem"].at[0]),
            pltpu.make_async_copy(r["q"], r["out_imom"], r["sem"].at[1]),
        ]

    rows = r["u"].shape[0] // ROW_CHUNKS

    def rows_out(k, u, p):
        part = pl.ds(k * rows, rows)
        return [
            pltpu.make_async_copy(u.at[part, :], r["out_users"].at[part, :], r["sem"].at[2 + 2 * k]),
            pltpu.make_async_copy(p.at[part, :], r["out_umom"].at[part, :], r["sem"].at[3 + 2 * k]),
        ]

    def finish(block):
        copies = items_out(block)
        for c in copies:
            c.start()
        for k in range(ROW_CHUNKS):
            part = slice(k * rows, (k + 1) * rows)
            p_new, u_new = user_rows(part, r["vo"][...], r["u"], r["p"], r["m"], r["rc"])
            r["ps"][part, :] = p_new
            r["us"][part, :] = u_new
            some = rows_out(k, r["us"], r["ps"])
            for c in some:
                c.start()
            copies += some
        for c in copies:
            c.wait()

    @pl.when(parity() == 1)
    def _():
        finish(pieces(r, "odd"))

    @pl.when(parity() == 0)
    def _():
        finish(pieces(r, "even"))


def body(ratings, rating_weights, user_counts, item_counts, users, user_moment, items, item_moment):
    n_outer = lax.axis_size("outer")
    n_inner = lax.axis_size("inner")
    width, rank = items.shape
    n_users = users.shape[0]
    block_of = lambda n: [jax.ShapeDtypeStruct((2 * rank // n, width), bf16)] * n
    icount = item_counts.reshape(-1, LANES)
    ucount = user_counts.reshape(-1, LANES)
    shapes = {
        "u": jax.ShapeDtypeStruct((n_users, rank), bf16),
        "ut": jax.ShapeDtypeStruct((rank, n_users), bf16),
        "p": jax.ShapeDtypeStruct((n_users, rank), f32),
        "m": jax.ShapeDtypeStruct((n_users, width), bf16),
        "vo": jax.ShapeDtypeStruct((rank, width), bf16),
        "rc": jax.ShapeDtypeStruct((n_users, LANES), f32),
    }
    early = {
        "xs": jax.ShapeDtypeStruct((n_users, width), bf16),
        "ws": jax.ShapeDtypeStruct((n_users, width), bf16),
        "cg": jax.ShapeDtypeStruct((8, LANES), jnp.int32),
    }
    numbered = lambda name, block: {name + str(k): (b, VMEM) for k, b in enumerate(block)}
    listed = lambda res, name: [res[name + str(k)] for k in range(len(res)) if name + str(k) in res]

    res = kernel_call(
        functools.partial(init_kernel, width),
        {
            "ratings": hbm(ratings), "weights": hbm(rating_weights), "icount": hbm(icount),
            "users": hbm(users), "umom": hbm(user_moment),
            "items": hbm(items), "imom": hbm(item_moment),
        },
        {
            **{n: (s, VMEM) for n, s in {**shapes, **early}.items()},
            **numbered("first", block_of(1)), **numbered("new", block_of(ODD_PIECES)),
        },
        {},
        [
            ("v", pltpu.VMEM((width, rank), bf16)),
            ("q", pltpu.VMEM((width, rank), bf16)),
            ("sem", pltpu.SemaphoreType.DMA((7,))),
        ],
    )
    state = {n: res[n] for n in STATE}
    odd_blk = even_blk = listed(res, "first")
    odd_new = listed(res, "new")

    tables = {"xs": (ratings, VMEM), "ws": (rating_weights, VMEM), "cg": (icount, VMEM)}
    first_tables = {n: (res[n], VMEM) for n in early}

    def item(item_parity, step, state, blk):
        sends_outer = step == STEPS // 2 - 1
        count = ODD_PIECES if item_parity == 1 or sends_outer else EVEN_PIECES
        res = kernel_call(
            functools.partial(item_kernel, width, item_parity, step),
            {
                **{n: (state[n], VMEM) for n in ("u", "ut", "m", "vo")},
                **(first_tables if step == 0 else tables),
                **numbered("blk", blk),
            },
            {**{n: (shapes[n], VMEM) for n in ("m", "vo")}, **numbered("new", block_of(count))},
            {n: n for n in ("m", "vo")},
        )
        return {**state, "m": res["m"], "vo": res["vo"]}, listed(res, "new")

    def user(step, state):
        changed = ("u", "ut", "p") + (("rc",) if step == 0 else ())
        res = kernel_call(
            functools.partial(user_kernel, step),
            {**{n: (state[n], VMEM) for n in STATE if n != "ut"}, "ut": (state["ut"], VMEM), "ucount": (ucount, VMEM)},
            {n: (shapes[n], VMEM) for n in changed},
            {n: n for n in changed},
            flops=USER_FLOPS,
        )
        return {**state, **res}

    for step in range(STEPS):
        if step > 0:
            state, odd_new = item(1, step, state, odd_blk)
        if step == STEPS // 2 - 1:
            odd_sent = shifted(odd_new, "outer", ring(n_outer))
        elif step < STEPS - 1:
            odd_sent = shifted(odd_new, "inner", ring(n_inner))
        state, even_new = item(0, step, state, even_blk)
        if step == STEPS // 2 - 1:
            odd_blk, even_blk = odd_sent, shifted(even_new, "outer", ring(n_outer))
        elif step < STEPS - 1:
            odd_blk, even_blk = shifted(even_new, "inner", swap(n_inner)), odd_sent
        if step < STEPS - 1:
            state = user(step, state)

    res = kernel_call(
        functools.partial(final_kernel, width),
        {
            **{n: (state[n], VMEM) for n in ("u", "p", "m", "vo", "rc")},
            **numbered("odd", odd_new), **numbered("even", even_new),
        },
        {
            "users": (shapes["u"], HBM), "umom": (shapes["p"], HBM),
            "items": (items, HBM), "imom": (items, HBM),
        },
        {},
        [
            ("v", pltpu.VMEM((width, rank), bf16)),
            ("q", pltpu.VMEM((width, rank), bf16)),
            ("us", pltpu.VMEM((n_users, rank), bf16)),
            ("ps", pltpu.VMEM((n_users, rank), f32)),
            ("sem", pltpu.SemaphoreType.DMA((2 + 2 * ROW_CHUNKS,))),
        ],
    )
    return (res["users"], res["umom"], res["items"], res["imom"])


def solution(mesh):
    in_specs = (
        P(("outer", "inner"), None),
        P(("outer", "inner"), None),
        P(("outer", "inner")),
        P(),
        P(("outer", "inner"), None),
        P(("outer", "inner"), None),
        P(("outer", "inner"), None),
        P(("outer", "inner"), None),
    )
    out_specs = (
        P(("outer", "inner"), None),
        P(("outer", "inner"), None),
        P(("outer", "inner"), None),
        P(("outer", "inner"), None),
    )
    return jax.shard_map(body, mesh=mesh, in_specs=in_specs, out_specs=out_specs, check_vma=False)
```

```python
import functools

import jax
import jax.numpy as jnp
from jax import lax
from jax.experimental import pallas as pl
from jax.experimental.pallas import tpu as pltpu
from jax.sharding import PartitionSpec as P

STEPS = 8
EARLY = 2
ODD_PIECES = 1
EVEN_PIECES = 2
USER_FLOPS = (1000, 3000000000)
LANES = 128
ROW_CHUNKS = 4

learn_rate = 0.3
moment_rate = 0.9
decay_rate = 0.02

f32 = jnp.float32
bf16 = jnp.bfloat16
VMEM = pltpu.MemorySpace.VMEM
HBM = pltpu.MemorySpace.HBM


def ring(count):
    return [(i, (i + 1) % count) for i in range(count)]


def swap(count):
    return [(i, i ^ 1) for i in range(count)]


def shifted(block, axis, pairs):
    return [lax.ppermute(piece, axis, pairs) for piece in block]


def hbm(array):
    return pltpu.with_memory_space_constraint(array, HBM), HBM


def kernel_call(kernel, ins, outs, aliases, scratch=(), flops=1000):
    names = list(ins) + ["out_" + n for n in outs] + [n for n, _ in scratch]

    def wrapped(*refs):
        kernel(dict(zip(names, refs)))

    in_names, out_names = list(ins), list(outs)
    res = pl.pallas_call(
        wrapped,
        out_shape=[jax.ShapeDtypeStruct(v[0].shape, v[0].dtype) for v in outs.values()],
        in_specs=[pl.BlockSpec(memory_space=v[1]) for v in ins.values()],
        out_specs=[pl.BlockSpec(memory_space=v[1]) for v in outs.values()],
        scratch_shapes=[s for _, s in scratch],
        input_output_aliases={in_names.index(a): out_names.index(b) for a, b in aliases.items()},
        compiler_params=pltpu.CompilerParams(vmem_limit_bytes=32 * 1024 * 1024),
        cost_estimate=pl.CostEstimate(flops=flops, bytes_accessed=1000, transcendentals=0),
    )(*[v[0] for v in ins.values()])
    return dict(zip(out_names, res))


def parity():
    return lax.rem(lax.axis_index("inner"), 2)


def anchor_of(step):
    n_outer, n_inner = lax.axis_size("outer"), lax.axis_size("inner")
    late = 1 if step >= STEPS // 2 else 0
    outer = lax.rem(lax.axis_index("outer") + (n_outer - late), n_outer)
    inner = lax.rem(lax.axis_index("inner") + (n_inner - (step - late)), n_inner)
    return outer * n_inner + inner


def first_copies(r, width):
    copies = []
    for name, out, base in (("ratings", "out_xs", 0), ("weights", "out_ws", EARLY)):
        for step in range(EARLY):
            cols = pl.ds(step * width, width)
            sem = r["sem"].at[base + step]
            copies.append(pltpu.make_async_copy(r[name].at[:, cols], r[out].at[:, cols], sem))
    for step in range(EARLY):
        group = pl.multiple_of(lax.div(anchor_of(step), 4) * 8, 8)
        rows = pl.ds(step * 8, 8)
        sem = r["sem"].at[2 * EARLY + step]
        copies.append(pltpu.make_async_copy(r["icount"].at[pl.ds(group, 8), :], r["out_cg"].at[rows, :], sem))
    return copies


def early_pair(cg, step):
    return cg[pl.ds(step * 8 + lax.rem(anchor_of(step), 4) * 2, 2), :]


def misfit_rows(part, cols, u, vt, xs, ws):
    pred = jnp.dot(u[part, :], vt, preferred_element_type=f32)
    x = xs[part, cols].astype(f32)
    return (ws[part, cols].astype(f32) * (pred - x)).astype(bf16)


def item_update(ut, vt, qt, pair, m):
    product = jnp.dot(ut[...], m[...], preferred_element_type=f32)
    pair = pair.astype(f32)
    inverse = 1.0 / jnp.concatenate([pair[0:1, :], pair[1:2, :]], axis=1)
    grad = product * inverse + decay_rate * vt.astype(f32)
    q_new = (moment_rate * qt.astype(f32) + grad).astype(bf16)
    v_new = (vt.astype(f32) - learn_rate * q_new.astype(f32)).astype(bf16)
    return v_new, q_new


def item_part(u, ut, vt, qt, xs, ws, cols, pair, m, vo, new):
    rows = u.shape[0] // ROW_CHUNKS
    for k in range(ROW_CHUNKS):
        part = slice(k * rows, (k + 1) * rows)
        m[part, :] = misfit_rows(part, cols, u, vt, xs, ws)
    v_new, q_new = item_update(ut, vt, qt, pair, m)
    put(new, v_new, q_new)
    vo[...] = vt


def user_rows(part, vt, u, p, m, rc):
    total = lax.dot_general(
        m[part, :], vt, (((1,), (1,)), ((), ())), preferred_element_type=f32
    )
    old = u[part, :].astype(f32)
    scale = jnp.concatenate([rc[part, :]] * (total.shape[1] // LANES), axis=1)
    p_new = moment_rate * p[part, :] + (total * scale + decay_rate * old)
    return p_new, (old - learn_rate * p_new).astype(bf16)


def put(block, vt, qt):
    if len(block) == 1:
        block[0][: vt.shape[0], :] = vt
        block[0][vt.shape[0] :, :] = qt
        return
    half = len(block) // 2
    span = vt.shape[0] // half
    for k in range(half):
        block[k][...] = vt[k * span : (k + 1) * span]
        block[half + k][...] = qt[k * span : (k + 1) * span]


def factors(block):
    if len(block) == 1:
        return block[0][: block[0].shape[0] // 2, :]
    return jnp.concatenate([ref[...] for ref in block[: len(block) // 2]], axis=0)


def momentum(block):
    if len(block) == 1:
        return block[0][block[0].shape[0] // 2 :, :]
    return jnp.concatenate([ref[...] for ref in block[len(block) // 2 :]], axis=0)


STATE = ("u", "ut", "p", "m", "vo", "rc")


def pieces(r, name):
    return [r[name + str(k)] for k in range(2 * len(r)) if name + str(k) in r]


def init_kernel(width, r):
    more = 3 * EARLY
    items = pltpu.make_async_copy(r["items"], r["v"], r["sem"].at[more])
    users = pltpu.make_async_copy(r["users"], r["out_u"], r["sem"].at[more + 1])
    imom = pltpu.make_async_copy(r["imom"], r["q"], r["sem"].at[more + 2])
    tables = first_copies(r, width)
    now = tables[::EARLY]
    later = [c for k, c in enumerate(tables) if k % EARLY]
    for c in [items, users, *now, imom, *later]:
        c.start()
    items.wait()
    vt = r["v"][...].T
    users.wait()
    r["out_ut"][...] = r["out_u"][...].T
    imom.wait()
    qt = r["q"][...].T
    first = pieces(r, "out_first")
    put(first, vt, qt)
    for c in now:
        c.wait()
    new = pieces(r, "out_new")

    @pl.when(parity() == 1)
    def _():
        item_part(
            r["out_u"], r["out_ut"], factors(first), momentum(first), r["out_xs"], r["out_ws"],
            slice(0, width), early_pair(r["out_cg"], 0), r["out_m"], r["out_vo"], new,
        )

    for c in later:
        c.wait()


def load_kernel(width, r):
    copies = [
        pltpu.make_async_copy(r["ratings"].at[:, pl.ds(EARLY * width, (STEPS - EARLY) * width)], r["out_xs"], r["sem"].at[0]),
        pltpu.make_async_copy(r["weights"].at[:, pl.ds(EARLY * width, (STEPS - EARLY) * width)], r["out_ws"], r["sem"].at[1]),
        pltpu.make_async_copy(r["icount"], r["out_cg"], r["sem"].at[2]),
    ]
    for c in copies:
        c.start()
    for c in copies:
        c.wait()


def step_tables(r, width, step):
    if step < EARLY:
        return slice(step * width, (step + 1) * width), early_pair(r["cg"], step)
    at = step - EARLY
    return slice(at * width, (at + 1) * width), r["cg"][pl.ds(anchor_of(step) * 2, 2), :]


def item_kernel(width, item_parity, step, r):
    @pl.when(parity() == item_parity)
    def _():
        blk = pieces(r, "blk")
        cols, pair = step_tables(r, width, step)
        item_part(
            r["u"], r["ut"], factors(blk), momentum(blk), r["xs"], r["ws"], cols, pair,
            r["out_m"], r["out_vo"], pieces(r, "out_new"),
        )


def user_kernel(step, r):
    if step == 0:
        inverse = 1.0 / r["ucount"][...].astype(f32)
        for k in range(inverse.shape[0]):
            row = jnp.broadcast_to(inverse[k : k + 1, :], (LANES, LANES))
            r["out_rc"][k * LANES : (k + 1) * LANES, :] = row.T
    rows = r["u"].shape[0] // ROW_CHUNKS
    for k in range(ROW_CHUNKS):
        part = slice(k * rows, (k + 1) * rows)
        p_new, u_new = user_rows(part, r["vo"][...], r["u"], r["p"], r["m"], r["out_rc"] if step == 0 else r["rc"])
        r["out_p"][part, :] = p_new
        r["out_u"][part, :] = u_new
        r["out_ut"][:, part] = u_new.T


def final_kernel(width, of, r):
    step = STEPS - 1
    cols, pair = step_tables(r, width, step)
    rows = r["u"].shape[0] // ROW_CHUNKS

    def finish(block):
        vt, qt = factors(block), momentum(block)
        copies = []
        for k in range(ROW_CHUNKS):
            part = slice(k * rows, (k + 1) * rows)
            r["ms"][part, :] = misfit_rows(part, cols, r["u"], vt, r["xs"], r["ws"])
            p_new, u_new = user_rows(part, vt, r["u"], r["p"], r["ms"], r["rc"])
            r["ps"][part, :] = p_new
            r["us"][part, :] = u_new
            span = pl.ds(k * rows, rows)
            some = [
                pltpu.make_async_copy(r["ps"].at[span, :], r["out_umom"].at[span, :], r["sem"].at[2 * k]),
                pltpu.make_async_copy(r["us"].at[span, :], r["out_users"].at[span, :], r["sem"].at[2 * k + 1]),
            ]
            for c in some:
                c.start()
            copies += some
        v_new, q_new = item_update(r["ut"], vt, qt, pair, r["ms"])
        r["v"][...] = v_new.T
        r["q"][...] = q_new.T
        last = [
            pltpu.make_async_copy(r["v"], r["out_items"], r["sem"].at[2 * ROW_CHUNKS]),
            pltpu.make_async_copy(r["q"], r["out_imom"], r["sem"].at[2 * ROW_CHUNKS + 1]),
        ]
        for c in last:
            c.start()
        for c in copies + last:
            c.wait()

    @pl.when(parity() == of)
    def _():
        finish(pieces(r, "blk"))


def body(ratings, rating_weights, user_counts, item_counts, users, user_moment, items, item_moment):
    n_outer = lax.axis_size("outer")
    n_inner = lax.axis_size("inner")
    width, rank = items.shape
    n_users = users.shape[0]
    block_of = lambda n: [jax.ShapeDtypeStruct((2 * rank // n, width), bf16)] * n
    icount = item_counts.reshape(-1, LANES)
    ucount = user_counts.reshape(-1, LANES)
    shapes = {
        "u": jax.ShapeDtypeStruct((n_users, rank), bf16),
        "ut": jax.ShapeDtypeStruct((rank, n_users), bf16),
        "p": jax.ShapeDtypeStruct((n_users, rank), f32),
        "m": jax.ShapeDtypeStruct((n_users, width), bf16),
        "vo": jax.ShapeDtypeStruct((rank, width), bf16),
        "rc": jax.ShapeDtypeStruct((n_users, LANES), f32),
    }
    early = {
        "xs": jax.ShapeDtypeStruct((n_users, EARLY * width), bf16),
        "ws": jax.ShapeDtypeStruct((n_users, EARLY * width), bf16),
        "cg": jax.ShapeDtypeStruct((8 * EARLY, LANES), jnp.int32),
    }
    late = {
        "xs": jax.ShapeDtypeStruct((n_users, (STEPS - EARLY) * width), bf16),
        "ws": jax.ShapeDtypeStruct((n_users, (STEPS - EARLY) * width), bf16),
        "cg": icount,
    }
    numbered = lambda name, block: {name + str(k): (b, VMEM) for k, b in enumerate(block)}
    listed = lambda res, name: [res[name + str(k)] for k in range(len(res)) if name + str(k) in res]

    res = kernel_call(
        functools.partial(init_kernel, width),
        {
            "ratings": hbm(ratings), "weights": hbm(rating_weights), "icount": hbm(icount),
            "users": hbm(users),
            "items": hbm(items), "imom": hbm(item_moment),
        },
        {
            **{n: (s, VMEM) for n, s in {**shapes, **early}.items() if n != "p"},
            **numbered("first", block_of(1)), **numbered("new", block_of(ODD_PIECES)),
        },
        {},
        [
            ("v", pltpu.VMEM((width, rank), bf16)),
            ("q", pltpu.VMEM((width, rank), bf16)),
            ("sem", pltpu.SemaphoreType.DMA((3 * EARLY + 3,))),
        ],
    )
    state = {n: res[n] for n in STATE if n != "p"}
    state["p"] = user_moment
    odd_blk = even_blk = listed(res, "first")
    odd_new = listed(res, "new")

    tables = {n: (res[n], VMEM) for n in early}

    def load(state):
        res = kernel_call(
            functools.partial(load_kernel, width),
            {
                "ratings": hbm(ratings), "weights": hbm(rating_weights), "icount": hbm(icount),
                "vo": (state["vo"], VMEM),
            },
            {**{n: (s, VMEM) for n, s in late.items()}, "vo": (shapes["vo"], VMEM)},
            {"vo": "vo"},
            [("sem", pltpu.SemaphoreType.DMA((3,)))],
        )
        return {**state, "vo": res["vo"]}, {n: (res[n], VMEM) for n in late}

    def item(item_parity, step, state, blk, tables):
        sends_outer = step == STEPS // 2 - 1
        late = 1 if step >= STEPS // 2 else 0
        count = EVEN_PIECES if item_parity == 0 and not sends_outer and (step + late) % 2 == 0 else ODD_PIECES
        res = kernel_call(
            functools.partial(item_kernel, width, item_parity, step),
            {
                **{n: (state[n], VMEM) for n in ("u", "ut", "m", "vo")},
                **tables,
                **numbered("blk", blk),
            },
            {**{n: (shapes[n], VMEM) for n in ("m", "vo")}, **numbered("new", block_of(count))},
            {n: n for n in ("m", "vo")},
        )
        return {**state, "m": res["m"], "vo": res["vo"]}, listed(res, "new")

    def user(step, state):
        changed = ("u", "ut", "p") + (("rc",) if step == 0 else ())
        res = kernel_call(
            functools.partial(user_kernel, step),
            {**{n: (state[n], VMEM) for n in STATE if n != "ut"}, "ut": (state["ut"], VMEM), "ucount": (ucount, VMEM)},
            {n: (shapes[n], VMEM) for n in changed},
            {n: n for n in changed if step > 0 or n != "p"},
            flops=USER_FLOPS[(step + (1 if step >= STEPS // 2 else 0)) % 2],
        )
        return {**state, **res}

    grid = [(o, i) for o in range(n_outer) for i in range(n_inner)]

    def outward(of):
        step_out = lambda o, i: (o + 1) % n_outer if i % 2 == of else o
        return [(o * n_inner + i, step_out(o, i) * n_inner + i) for o, i in grid]

    both = ("outer", "inner")
    for step in range(STEPS - 1):
        turn = step == STEPS // 2 - 1
        if step > 0:
            state, odd_new = item(1, step, state, odd_blk, tables)
        early_tables = tables
        if step == EARLY - 1:
            state, tables = load(state)
        odd_sent = shifted(odd_new, both, outward(1)) if turn else shifted(odd_new, "inner", ring(n_inner))
        state, even_new = item(0, step, state, even_blk, early_tables)
        if turn:
            odd_blk, even_blk = odd_sent, shifted(even_new, both, outward(0))
        else:
            odd_blk, even_blk = shifted(even_new, "inner", swap(n_inner)), odd_sent
        state = user(step, state)

    def final(of, blk, base):
        outs = {
            "users": (shapes["u"], HBM), "umom": (shapes["p"], HBM),
            "items": (items, HBM), "imom": (items, HBM),
        }
        return kernel_call(
            functools.partial(final_kernel, width, of),
            {
                **{n: (state[n], VMEM) for n in ("u", "ut", "p", "rc")}, **tables, **numbered("blk", blk),
                **{"base_" + n: hbm(b) for n, b in base.items()},
            },
            outs,
            {"base_" + n: n for n in base},
            [
                ("v", pltpu.VMEM((width, rank), bf16)),
                ("q", pltpu.VMEM((width, rank), bf16)),
                ("us", pltpu.VMEM((n_users, rank), bf16)),
                ("ps", pltpu.VMEM((n_users, rank), f32)),
                ("ms", pltpu.VMEM((n_users, width), bf16)),
                ("sem", pltpu.SemaphoreType.DMA((2 + 2 * ROW_CHUNKS,))),
            ],
        )

    res = final(0, even_blk, final(1, odd_blk, {}))
    return (res["users"], res["umom"], res["items"], res["imom"])


def solution(mesh):
    in_specs = (
        P(("outer", "inner"), None),
        P(("outer", "inner"), None),
        P(("outer", "inner")),
        P(),
        P(("outer", "inner"), None),
        P(("outer", "inner"), None),
        P(("outer", "inner"), None),
        P(("outer", "inner"), None),
    )
    out_specs = (
        P(("outer", "inner"), None),
        P(("outer", "inner"), None),
        P(("outer", "inner"), None),
        P(("outer", "inner"), None),
    )
    return jax.shard_map(body, mesh=mesh, in_specs=in_specs, out_specs=out_specs, check_vma=False)
```

```python
import functools

import jax
import jax.numpy as jnp
from jax import lax
from jax.experimental import pallas as pl
from jax.experimental.pallas import tpu as pltpu
from jax.sharding import PartitionSpec as P

STEPS = 8
EARLY = 2
ODD_PIECES = 1
EVEN_PIECES = 2
USER_FLOPS = (1000, 3000000000)
LANES = 128
ROW_CHUNKS = 4

learn_rate = 0.3
moment_rate = 0.9
decay_rate = 0.02

f32 = jnp.float32
bf16 = jnp.bfloat16
VMEM = pltpu.MemorySpace.VMEM
HBM = pltpu.MemorySpace.HBM


def ring(count):
    return [(i, (i + 1) % count) for i in range(count)]


def swap(count):
    return [(i, i ^ 1) for i in range(count)]


def shifted(block, axis, pairs):
    return [lax.ppermute(piece, axis, pairs) for piece in block]


def hbm(array):
    return pltpu.with_memory_space_constraint(array, HBM), HBM


def kernel_call(kernel, ins, outs, aliases, scratch=(), flops=1000):
    names = list(ins) + ["out_" + n for n in outs] + [n for n, _ in scratch]

    def wrapped(*refs):
        kernel(dict(zip(names, refs)))

    in_names, out_names = list(ins), list(outs)
    res = pl.pallas_call(
        wrapped,
        out_shape=[jax.ShapeDtypeStruct(v[0].shape, v[0].dtype) for v in outs.values()],
        in_specs=[pl.BlockSpec(memory_space=v[1]) for v in ins.values()],
        out_specs=[pl.BlockSpec(memory_space=v[1]) for v in outs.values()],
        scratch_shapes=[s for _, s in scratch],
        input_output_aliases={in_names.index(a): out_names.index(b) for a, b in aliases.items()},
        compiler_params=pltpu.CompilerParams(vmem_limit_bytes=32 * 1024 * 1024),
        cost_estimate=pl.CostEstimate(flops=flops, bytes_accessed=1000, transcendentals=0),
    )(*[v[0] for v in ins.values()])
    return dict(zip(out_names, res))


def parity():
    return lax.rem(lax.axis_index("inner"), 2)


def anchor_of(step):
    n_outer, n_inner = lax.axis_size("outer"), lax.axis_size("inner")
    late = 1 if step >= STEPS // 2 else 0
    outer = lax.rem(lax.axis_index("outer") + (n_outer - late), n_outer)
    inner = lax.rem(lax.axis_index("inner") + (n_inner - (step - late)), n_inner)
    return outer * n_inner + inner


def first_copies(r, width):
    copies = []
    for name, out, base in (("ratings", "out_xs", 0), ("weights", "out_ws", EARLY)):
        for step in range(EARLY):
            cols = pl.ds(step * width, width)
            sem = r["sem"].at[base + step]
            copies.append(pltpu.make_async_copy(r[name].at[:, cols], r[out].at[:, cols], sem))
    for step in range(EARLY):
        group = pl.multiple_of(lax.div(anchor_of(step), 4) * 8, 8)
        rows = pl.ds(step * 8, 8)
        sem = r["sem"].at[2 * EARLY + step]
        copies.append(pltpu.make_async_copy(r["icount"].at[pl.ds(group, 8), :], r["out_cg"].at[rows, :], sem))
    return copies


def early_pair(cg, step):
    return cg[pl.ds(step * 8 + lax.rem(anchor_of(step), 4) * 2, 2), :]


def misfit_rows(part, cols, u, vt, xs, ws):
    pred = jnp.dot(u[part, :], vt, preferred_element_type=f32)
    x = xs[part, cols].astype(f32)
    return (ws[part, cols].astype(f32) * (pred - x)).astype(bf16)


def item_update(ut, vt, qt, pair, m):
    product = jnp.dot(ut[...], m[...], preferred_element_type=f32)
    pair = pair.astype(f32)
    inverse = 1.0 / jnp.concatenate([pair[0:1, :], pair[1:2, :]], axis=1)
    grad = product * inverse + decay_rate * vt.astype(f32)
    q_new = (moment_rate * qt.astype(f32) + grad).astype(bf16)
    v_new = (vt.astype(f32) - learn_rate * q_new.astype(f32)).astype(bf16)
    return v_new, q_new


def item_part(u, ut, vt, qt, xs, ws, cols, pair, m, vo, new):
    rows = u.shape[0] // ROW_CHUNKS
    for k in range(ROW_CHUNKS):
        part = slice(k * rows, (k + 1) * rows)
        m[part, :] = misfit_rows(part, cols, u, vt, xs, ws)
    v_new, q_new = item_update(ut, vt, qt, pair, m)
    put(new, v_new, q_new)
    vo[...] = vt


def user_rows(part, vt, u, p, m, rc):
    total = lax.dot_general(
        m[part, :], vt, (((1,), (1,)), ((), ())), preferred_element_type=f32
    )
    old = u[part, :].astype(f32)
    scale = jnp.concatenate([rc[part, :]] * (total.shape[1] // LANES), axis=1)
    p_new = moment_rate * p[part, :] + (total * scale + decay_rate * old)
    return p_new, (old - learn_rate * p_new).astype(bf16)


def put(block, vt, qt):
    if len(block) == 1:
        block[0][: vt.shape[0], :] = vt
        block[0][vt.shape[0] :, :] = qt
        return
    half = len(block) // 2
    span = vt.shape[0] // half
    for k in range(half):
        block[k][...] = vt[k * span : (k + 1) * span]
        block[half + k][...] = qt[k * span : (k + 1) * span]


def factors(block):
    if len(block) == 1:
        return block[0][: block[0].shape[0] // 2, :]
    return jnp.concatenate([ref[...] for ref in block[: len(block) // 2]], axis=0)


def momentum(block):
    if len(block) == 1:
        return block[0][block[0].shape[0] // 2 :, :]
    return jnp.concatenate([ref[...] for ref in block[len(block) // 2 :]], axis=0)


STATE = ("u", "ut", "p", "m", "vo", "rc")


def pieces(r, name):
    return [r[name + str(k)] for k in range(2 * len(r)) if name + str(k) in r]


def init_kernel(width, r):
    more = 3 * EARLY
    items = pltpu.make_async_copy(r["items"], r["v"], r["sem"].at[more])
    users = pltpu.make_async_copy(r["users"], r["out_u"], r["sem"].at[more + 1])
    imom = pltpu.make_async_copy(r["imom"], r["q"], r["sem"].at[more + 2])
    tables = first_copies(r, width)
    now = tables[::EARLY]
    later = [c for k, c in enumerate(tables) if k % EARLY]
    for c in [items, users, *now, imom]:
        c.start()

    @pl.when(parity() == 1)
    def _():
        for c in later:
            c.start()

    items.wait()
    vt = r["v"][...].T
    users.wait()
    r["out_ut"][...] = r["out_u"][...].T
    imom.wait()
    qt = r["q"][...].T
    first = pieces(r, "out_first")
    put(first, vt, qt)
    for c in now:
        c.wait()
    new = pieces(r, "out_new")

    @pl.when(parity() == 1)
    def _():
        item_part(
            r["out_u"], r["out_ut"], factors(first), momentum(first), r["out_xs"], r["out_ws"],
            slice(0, width), early_pair(r["out_cg"], 0), r["out_m"], r["out_vo"], new,
        )
        for c in later:
            c.wait()


def load_kernel(width, r):
    copies = [
        pltpu.make_async_copy(r["ratings"].at[:, pl.ds(width, (STEPS - 1) * width)], r["out_xs"], r["sem"].at[0]),
        pltpu.make_async_copy(r["weights"].at[:, pl.ds(width, (STEPS - 1) * width)], r["out_ws"], r["sem"].at[1]),
        pltpu.make_async_copy(r["icount"], r["out_cg"], r["sem"].at[2]),
    ]
    for c in copies:
        c.start()
    for c in copies:
        c.wait()


def step_tables(r, width, step, early=False):
    if early:
        return slice(step * width, (step + 1) * width), early_pair(r["cg"], step)
    return slice((step - 1) * width, step * width), r["cg"][pl.ds(anchor_of(step) * 2, 2), :]


def item_kernel(width, item_parity, step, r):
    @pl.when(parity() == item_parity)
    def _():
        blk = pieces(r, "blk")
        early = step == 0 or (step < EARLY and item_parity == 1)
        cols, pair = step_tables(r, width, step, early)
        item_part(
            r["u"], r["ut"], factors(blk), momentum(blk), r["xs"], r["ws"], cols, pair,
            r["out_m"], r["out_vo"], pieces(r, "out_new"),
        )


def user_kernel(step, r):
    if step == 0:
        inverse = 1.0 / r["ucount"][...].astype(f32)
        for k in range(inverse.shape[0]):
            row = jnp.broadcast_to(inverse[k : k + 1, :], (LANES, LANES))
            r["out_rc"][k * LANES : (k + 1) * LANES, :] = row.T
    rows = r["u"].shape[0] // ROW_CHUNKS
    for k in range(ROW_CHUNKS):
        part = slice(k * rows, (k + 1) * rows)
        p_new, u_new = user_rows(part, r["vo"][...], r["u"], r["p"], r["m"], r["out_rc"] if step == 0 else r["rc"])
        r["out_p"][part, :] = p_new
        r["out_u"][part, :] = u_new
        r["out_ut"][:, part] = u_new.T


def final_kernel(width, of, r):
    step = STEPS - 1
    cols, pair = step_tables(r, width, step)
    rows = r["u"].shape[0] // ROW_CHUNKS

    def finish(block):
        vt, qt = factors(block), momentum(block)
        copies = []
        for k in range(ROW_CHUNKS):
            part = slice(k * rows, (k + 1) * rows)
            r["ms"][part, :] = misfit_rows(part, cols, r["u"], vt, r["xs"], r["ws"])
            p_new, u_new = user_rows(part, vt, r["u"], r["p"], r["ms"], r["rc"])
            r["ps"][part, :] = p_new
            r["us"][part, :] = u_new
            span = pl.ds(k * rows, rows)
            some = [
                pltpu.make_async_copy(r["ps"].at[span, :], r["out_umom"].at[span, :], r["sem"].at[2 * k]),
                pltpu.make_async_copy(r["us"].at[span, :], r["out_users"].at[span, :], r["sem"].at[2 * k + 1]),
            ]
            for c in some:
                c.start()
            copies += some
        v_new, q_new = item_update(r["ut"], vt, qt, pair, r["ms"])
        r["v"][...] = v_new.T
        r["q"][...] = q_new.T
        last = [
            pltpu.make_async_copy(r["v"], r["out_items"], r["sem"].at[2 * ROW_CHUNKS]),
            pltpu.make_async_copy(r["q"], r["out_imom"], r["sem"].at[2 * ROW_CHUNKS + 1]),
        ]
        for c in last:
            c.start()
        for c in copies + last:
            c.wait()

    @pl.when(parity() == of)
    def _():
        finish(pieces(r, "blk"))


def body(ratings, rating_weights, user_counts, item_counts, users, user_moment, items, item_moment):
    n_outer = lax.axis_size("outer")
    n_inner = lax.axis_size("inner")
    width, rank = items.shape
    n_users = users.shape[0]
    block_of = lambda n: [jax.ShapeDtypeStruct((2 * rank // n, width), bf16)] * n
    icount = item_counts.reshape(-1, LANES)
    ucount = user_counts.reshape(-1, LANES)
    shapes = {
        "u": jax.ShapeDtypeStruct((n_users, rank), bf16),
        "ut": jax.ShapeDtypeStruct((rank, n_users), bf16),
        "p": jax.ShapeDtypeStruct((n_users, rank), f32),
        "m": jax.ShapeDtypeStruct((n_users, width), bf16),
        "vo": jax.ShapeDtypeStruct((rank, width), bf16),
        "rc": jax.ShapeDtypeStruct((n_users, LANES), f32),
    }
    early = {
        "xs": jax.ShapeDtypeStruct((n_users, EARLY * width), bf16),
        "ws": jax.ShapeDtypeStruct((n_users, EARLY * width), bf16),
        "cg": jax.ShapeDtypeStruct((8 * EARLY, LANES), jnp.int32),
    }
    late = {
        "xs": jax.ShapeDtypeStruct((n_users, (STEPS - 1) * width), bf16),
        "ws": jax.ShapeDtypeStruct((n_users, (STEPS - 1) * width), bf16),
        "cg": icount,
    }
    numbered = lambda name, block: {name + str(k): (b, VMEM) for k, b in enumerate(block)}
    listed = lambda res, name: [res[name + str(k)] for k in range(len(res)) if name + str(k) in res]

    res = kernel_call(
        functools.partial(init_kernel, width),
        {
            "ratings": hbm(ratings), "weights": hbm(rating_weights), "icount": hbm(icount),
            "users": hbm(users),
            "items": hbm(items), "imom": hbm(item_moment),
        },
        {
            **{n: (s, VMEM) for n, s in {**shapes, **early}.items() if n != "p"},
            **numbered("first", block_of(1)), **numbered("new", block_of(ODD_PIECES)),
        },
        {},
        [
            ("v", pltpu.VMEM((width, rank), bf16)),
            ("q", pltpu.VMEM((width, rank), bf16)),
            ("sem", pltpu.SemaphoreType.DMA((3 * EARLY + 3,))),
        ],
    )
    state = {n: res[n] for n in STATE if n != "p"}
    state["p"] = user_moment
    odd_blk = even_blk = listed(res, "first")
    odd_new = listed(res, "new")

    tables = {n: (res[n], VMEM) for n in early}

    def load(state):
        res = kernel_call(
            functools.partial(load_kernel, width),
            {
                "ratings": hbm(ratings), "weights": hbm(rating_weights), "icount": hbm(icount),
                "vo": (state["vo"], VMEM),
            },
            {**{n: (s, VMEM) for n, s in late.items()}, "vo": (shapes["vo"], VMEM)},
            {"vo": "vo"},
            [("sem", pltpu.SemaphoreType.DMA((3,)))],
        )
        return {**state, "vo": res["vo"]}, {n: (res[n], VMEM) for n in late}

    def item(item_parity, step, state, blk, tables):
        sends_outer = step == STEPS // 2 - 1
        late = 1 if step >= STEPS // 2 else 0
        count = EVEN_PIECES if item_parity == 0 and not sends_outer and (step + late) % 2 == 0 else ODD_PIECES
        res = kernel_call(
            functools.partial(item_kernel, width, item_parity, step),
            {
                **{n: (state[n], VMEM) for n in ("u", "ut", "m", "vo")},
                **tables,
                **numbered("blk", blk),
            },
            {**{n: (shapes[n], VMEM) for n in ("m", "vo")}, **numbered("new", block_of(count))},
            {n: n for n in ("m", "vo")},
        )
        return {**state, "m": res["m"], "vo": res["vo"]}, listed(res, "new")

    def user(step, state):
        changed = ("u", "ut", "p") + (("rc",) if step == 0 else ())
        res = kernel_call(
            functools.partial(user_kernel, step),
            {**{n: (state[n], VMEM) for n in STATE if n != "ut"}, "ut": (state["ut"], VMEM), "ucount": (ucount, VMEM)},
            {n: (shapes[n], VMEM) for n in changed},
            {n: n for n in changed if step > 0 or n != "p"},
            flops=USER_FLOPS[(step + (1 if step >= STEPS // 2 else 0)) % 2],
        )
        return {**state, **res}

    grid = [(o, i) for o in range(n_outer) for i in range(n_inner)]

    def outward(of):
        step_out = lambda o, i: (o + 1) % n_outer if i % 2 == of else o
        return [(o * n_inner + i, step_out(o, i) * n_inner + i) for o, i in grid]

    both = ("outer", "inner")
    for step in range(STEPS - 1):
        turn = step == STEPS // 2 - 1
        if step > 0:
            state, odd_new = item(1, step, state, odd_blk, tables)
        if step == EARLY - 1:
            state, tables = load(state)
        odd_sent = shifted(odd_new, both, outward(1)) if turn else shifted(odd_new, "inner", ring(n_inner))
        state, even_new = item(0, step, state, even_blk, tables)
        if turn:
            odd_blk, even_blk = odd_sent, shifted(even_new, both, outward(0))
        else:
            odd_blk, even_blk = shifted(even_new, "inner", swap(n_inner)), odd_sent
        state = user(step, state)

    def final(of, blk, base):
        outs = {
            "users": (shapes["u"], HBM), "umom": (shapes["p"], HBM),
            "items": (items, HBM), "imom": (items, HBM),
        }
        return kernel_call(
            functools.partial(final_kernel, width, of),
            {
                **{n: (state[n], VMEM) for n in ("u", "ut", "p", "rc")}, **tables, **numbered("blk", blk),
                **{"base_" + n: hbm(b) for n, b in base.items()},
            },
            outs,
            {"base_" + n: n for n in base},
            [
                ("v", pltpu.VMEM((width, rank), bf16)),
                ("q", pltpu.VMEM((width, rank), bf16)),
                ("us", pltpu.VMEM((n_users, rank), bf16)),
                ("ps", pltpu.VMEM((n_users, rank), f32)),
                ("ms", pltpu.VMEM((n_users, width), bf16)),
                ("sem", pltpu.SemaphoreType.DMA((2 + 2 * ROW_CHUNKS,))),
            ],
        )

    res = final(0, even_blk, final(1, odd_blk, {}))
    return (res["users"], res["umom"], res["items"], res["imom"])


def solution(mesh):
    in_specs = (
        P(("outer", "inner"), None),
        P(("outer", "inner"), None),
        P(("outer", "inner")),
        P(),
        P(("outer", "inner"), None),
        P(("outer", "inner"), None),
        P(("outer", "inner"), None),
        P(("outer", "inner"), None),
    )
    out_specs = (
        P(("outer", "inner"), None),
        P(("outer", "inner"), None),
        P(("outer", "inner"), None),
        P(("outer", "inner"), None),
    )
    return jax.shard_map(body, mesh=mesh, in_specs=in_specs, out_specs=out_specs, check_vma=False)
```
